128 devices in a mesh: wide: 16 (over z, y), narrow: 8 (over x, core).
Axes of the slice: x: 4, y: 4, z: 4, core: 2. Of those that a mesh axis runs over, the one named last changes fastest.
Arguments:
- state: bfloat16 [4096, 1024, 128], P(('wide', 'narrow')), may hold values from -6 to 6
- group_of: int32 [4096], replicated, may hold values from 0 to 4095, as said below
- w_in: bfloat16 [1024, 1024], replicated, may hold values from -0.1875 to 0.1875
- w_out: bfloat16 [1024, 1024], replicated, may hold values from -0.1875 to 0.1875
- w_flux: bfloat16 [32, 1024], replicated, may hold values from -0.1875 to 0.1875
- owner: int32 [524288, 1], P(('wide', 'narrow')), may hold values from 0 to 127; in each aligned block of 4096 rows (0 to 4095, 4096 to 8191, ...) at most 64 rows name the same one
- ocean_slot: int32 [524288], P(('wide', 'narrow')), may hold values from 0 to 511
- remap_weight: float32 [524288], P(('wide', 'narrow')), may hold values from 0.25 to 4
Outputs:
- new_state: bfloat16 [4096, 1024, 128], P(('wide', 'narrow'))
- ocean: float32 [32, 65536], P(None, ('wide', 'narrow'))
The draws below stay inside these ranges and needn't reach their ends.
Inputs may be any that keep to these rules, and one draw needn't show every extreme that they name: group_of is a permutation of the blocks. Block p = ((w * 8 + n) * 32 + s) keeps n and s; for each n exactly 8 slots s move, each to wide index (w + c) modulo the wide size with a nonzero c of its own, and all other blocks stay.
All inputs are finite; a program needn't handle non-finite values.
Results may differ from the reference program's by a relative error of at most 0.0044.
Values may be sent and summed in bfloat16 or wider, within the bound.
A program may use at most 192 MiB of HBM per device.

```python
import math
import jax
import jax.numpy as jnp
import numpy as np
from jax import lax

LEV = 128
VARS = 8
HID = 1024
NFLUX = 32
COLS = 128
BLK_DEV = 32
OCN_DEV = 512
MOVE = 8
NBLK = 4096
OCEANS = 65536
CAP = 64
N_WIDE = 16
N_NARROW = 8
DEVICES = 128


def draw_group_of(key, part):
    keys = jax.random.split(jax.random.fold_in(key, 11), N_NARROW)

    def band_shifts(band_key):
        first, second = jax.random.split(band_key)
        order = jax.random.permutation(first, BLK_DEV)
        shifts = jax.random.permutation(second, N_WIDE - 1)[:MOVE].astype(jnp.int32) + 1
        return jnp.zeros((BLK_DEV,), jnp.int32).at[order[:MOVE]].set(shifts)
    shift_table = jax.vmap(band_shifts)(keys)
    wide_idx = jnp.arange(N_WIDE, dtype=jnp.int32)[:, None, None]
    band_idx = jnp.arange(N_NARROW, dtype=jnp.int32)[None, :, None]
    slot_idx = jnp.arange(BLK_DEV, dtype=jnp.int32)[None, None, :]
    target_wide = (wide_idx + shift_table[None, :, :]) % N_WIDE
    dest = (target_wide * N_NARROW + band_idx) * BLK_DEV + slot_idx
    return dest.reshape(-1).astype(jnp.int32)


def place_ends(entries, rng, least, largest):
    extent = entries.shape
    spot = [jax.random.randint(jax.random.fold_in(rng, axis), (), 0, extent[axis]) for axis in range(len(extent))]
    entries = entries.at[tuple(spot)].set(least)
    longest = extent.index(max(extent))
    spot[longest] = (spot[longest] + 1) % extent[longest]
    return entries.at[tuple(spot)].set(largest)


def level_of(own_key, extent, shards, least, high):
    gain = 1.0
    for dim, shards_of in shards:
        heights = jax.random.uniform(jax.random.fold_in(jax.random.fold_in(own_key, 6), dim), (shards_of,), jnp.float32, least / len(shards), high / len(shards))
        gain = gain * jnp.repeat(jnp.exp(heights), extent[dim] // shards_of).reshape((-1,) + (1,) * (len(extent) - 1 - dim))
    return gain


def shared_out(own_key, own, number, rows, amount, top, limit, skew):
    ranking = jax.random.permutation(own_key, amount)
    crowded, common = shares(amount, rows * top, limit, skew, True), shares(amount, rows * top, limit, skew, False)
    places = jnp.arange(amount)

    def named(tallies, rotation):
        used = int((tallies > 0).sum())
        fixed = max(1, used // 4)
        shifted = fixed + (places - fixed + rotation * (used - fixed)) % max(1, amount - fixed)
        return jnp.zeros((amount,), jnp.int32).at[ranking[jnp.where(places < fixed, places, shifted)]].set(jnp.asarray(tallies, jnp.int32))

    tallies = jnp.where(number % 4 == 0, named(crowded, number // 4), named(common, number - number // 4 - 1))
    mixed = jax.random.permutation(jax.random.fold_in(own, 3), amount)
    donor, receiver = mixed[0:amount // 2 * 2:2], mixed[1:amount // 2 * 2:2]
    room = jnp.minimum(tallies[donor] - 1, limit - tallies[receiver]) // 2
    room = jnp.where((donor == ranking[0]) | (receiver == ranking[0]) | (tallies[receiver] == 0), 0, jnp.maximum(room, 0))
    shifted = jax.random.randint(jax.random.fold_in(own, 4), (amount // 2,), 0, 1 << 20) % (room + 1)
    tallies = tallies.at[donor].add(-shifted).at[receiver].add(shifted)
    members = jnp.searchsorted(jnp.cumsum(tallies), jnp.arange(rows * top), side="right").astype(jnp.int32)
    table = members.reshape(top, rows).T
    table = table[jax.random.permutation(jax.random.fold_in(own, 1), rows)]
    rotation = jax.random.randint(jax.random.fold_in(own, 2), (rows, 1), 0, top)
    return jnp.take_along_axis(table, (jnp.arange(top)[None, :] + rotation) % top, axis=1)


def shares(amount, total, reach, lean, full):
    portions = [(1 << 20) // math.isqrt(grade ** lean) + 1 for grade in range(1, amount + 1)]
    largest = reach if full else min(reach, max(-(-total // amount), total * portions[0] // sum(portions)))
    least = 1 if total - largest >= amount - 1 else 0
    given, rest = [largest] + [least] * (amount - 1), total - largest - least * (amount - 1)
    while rest > 0:
        candidates = [i for i in range(1, amount) if given[i] < largest] or [i for i in range(1, amount) if given[i] < reach]
        mass, left = sum([portions[i] for i in candidates]), rest
        for i in candidates:
            addition = min(reach - given[i], max(1, left * portions[i] // mass), rest)
            given[i] = given[i] + addition
            rest = rest - addition
    return np.array(given)


def gaussian(own_key, shape, scale, bound, shards=(), kind=jnp.bfloat16):
    factor_of = level_of(own_key, shape, shards, -0.22, 0.18) if shards else 1.0
    array = jax.random.normal(own_key, shape, jnp.float32) * scale * factor_of
    return jnp.minimum(jnp.maximum(array, -bound), bound).astype(kind)


def setup_inputs(seed: int = 0) -> dict:
    key_list = jax.random.split(jax.random.key(seed), 9)
    state = gaussian(key_list[0], (NBLK, VARS * LEV, COLS), 1.0, 6.0, ((0, 128),))
    group_of = draw_group_of(jax.random.fold_in(key_list[8], 71), 0)
    w_in = gaussian(key_list[2], (HID, VARS * LEV), (VARS * LEV) ** -0.5, 0.1875)
    w_out = gaussian(key_list[3], (VARS * LEV, HID), HID ** -0.5, 0.1875)
    w_flux = gaussian(key_list[4], (NFLUX, HID), HID ** -0.5, 0.1875)
    owner_keys = jax.random.split(jax.random.fold_in(key_list[5], 1), (NBLK * COLS) // (BLK_DEV * COLS))
    owner_turns = jax.random.permutation(jax.random.fold_in(key_list[5], 3), (NBLK * COLS) // (BLK_DEV * COLS))
    owner = jax.vmap(lambda own, number: shared_out(jax.random.fold_in(key_list[5], 2), own, number, BLK_DEV * COLS, DEVICES, 1, CAP, 2))(owner_keys, owner_turns).reshape((NBLK * COLS, 1))
    ocean_slot = place_ends(jax.random.randint(key_list[6], (NBLK * COLS,), 0, OCN_DEV), jax.random.fold_in(key_list[6], 1), 0, OCN_DEV - 1).astype(jnp.int32)
    remap_weight = jnp.clip(jnp.exp(math.log(4.0) - 2.7725887 * jax.random.uniform(key_list[7], (NBLK * COLS,), jnp.float32) ** level_of(key_list[7], (NBLK * COLS,), ((0, 128),), -0.2, 0.2)), 0.25, 4.0)
    return dict(state=state, group_of=group_of, w_in=w_in, w_out=w_out, w_flux=w_flux, owner=owner, ocean_slot=ocean_slot, remap_weight=remap_weight)


def reference(state, group_of, w_in, w_out, w_flux, owner, ocean_slot, remap_weight):
    group = jnp.zeros_like(state).at[group_of].set(state)

    def one_block(block):
        hidden = jax.nn.silu(jnp.dot(w_in, block, preferred_element_type=jnp.float32)).astype(jnp.bfloat16)
        fresh = (block.astype(jnp.float32) + jnp.dot(w_out, hidden, preferred_element_type=jnp.float32)).astype(jnp.bfloat16)
        surface = jnp.dot(w_flux, hidden, preferred_element_type=jnp.float32)
        return fresh, surface

    new_state, surface = lax.map(one_block, group)
    flux = jnp.transpose(surface, (1, 0, 2)).reshape(NFLUX, NBLK * COLS) * remap_weight[None, :]
    target = owner[:, 0] * OCN_DEV + ocean_slot
    ocean = jnp.zeros((NFLUX, OCEANS), jnp.float32).at[:, target].add(flux)
    return new_state, ocean
```

```python
import functools

import jax
import jax.numpy as jnp
from jax import lax
from jax.experimental import pallas as pl
from jax.experimental.pallas import tpu as pltpu
from jax.sharding import PartitionSpec as P

F32, BF16, I32 = jnp.float32, jnp.bfloat16, jnp.int32
MESH = pl.DeviceIdType.MESH
NT = (((1,), (1,)), ((), ()))

BLOCKS, DEPTH, COLS = 32, 1024, 128
NFLUX, SLOTS = 32, 512
WIDE, NARROW, SIDE = 16, 8, 4
DEVICES = WIDE * NARROW
MOVE, STAY = 8, 24
GROUP = 4
CHUNK = 256
ITEMS = (
    (1, 0), (3, 0), (0, 1), (0, 3), (2, 2), (1, 1), (3, 3), (1, 3),
    (3, 1), (2, 1), (2, 3), (1, 2), (3, 2), (2, 0), (0, 2),
)
CODES = tuple(dz * SIDE + dy for dy, dz in ITEMS)
EARLY = 11
PARTS = 4


def silu(v):
    return v / (1.0 + jnp.exp(-v))


def main_kernel(
    group_of, state, w_in_hbm, w_out_hbm, w_flux, owner, slot, weight,
    pool, ocean, sel,
    xs, ys, send, w_in, w_out, hid, fm, fs, fp, key, jrank, bmat, msg, n1, w2, sl, s1, s1t, s2, hot,
    code_t, slot_t, next_t, rank_t, order_t, local_t,
    load_sem, pool_sem, big_s, big_r, fl_s, fl_r, na_s, na_r, wi_s, wi_r, sn_s, sn_r, sw_s, sw_r,
):
    w, n = lax.axis_index("wide"), lax.axis_index("narrow")
    y, z = lax.rem(w, SIDE), lax.div(w, SIDE)
    loads = [
        pltpu.make_async_copy(w_in_hbm, w_in, load_sem.at[0]),
        pltpu.make_async_copy(w_out_hbm, w_out, load_sem.at[9]),
    ]
    for i in range(8):
        loads.append(
            pltpu.make_async_copy(
                state.at[pl.ds(4 * i, 4)], xs.at[pl.ds(4 * i, 4)], load_sem.at[1 + i]
            )
        )
    loads[0].start()
    for c in loads[2:]:
        c.start()
    loads[1].start()

    def target(p):
        dy, dz = ITEMS[p]
        return (lax.rem(z + dz, SIDE) * SIDE + lax.rem(y + dy, SIDE), n)

    wide_peers = [(lax.rem(w + d, WIDE), n) for d in range(1, WIDE)]
    narrow_peers = [(w, lax.rem(n + d, NARROW)) for d in range(1, NARROW)]
    barrier = pltpu.get_barrier_semaphore()
    for peer in wide_peers + narrow_peers:
        pl.semaphore_signal(barrier, inc=1, device_id=peer, device_id_type=MESH)

    base_row = (w * NARROW + n) * BLOCKS

    def scan_slots(s, found):
        t = lax.div(group_of[base_row + s], NARROW * BLOCKS)
        dy = lax.rem(lax.rem(t, SIDE) - y + SIDE, SIDE)
        dz = lax.rem(lax.div(t, SIDE) - z + SIDE, SIDE)
        src = lax.rem(2 * w - t + 2 * WIDE, WIDE)
        ry = lax.rem(y - lax.rem(src, SIDE) + SIDE, SIDE)
        rz = lax.rem(z - lax.div(src, SIDE) + SIDE, SIDE)
        code = dz * SIDE + dy
        code_t[s] = code
        sel[s] = STAY + rz * SIDE + ry
        return tuple(jnp.where(code == CODES[p], s, found[p]) for p in range(15))

    found = lax.fori_loop(0, BLOCKS, scan_slots, (jnp.int32(-1),) * 15)
    nxt = jnp.int32(15)
    slot_t[15] = jnp.int32(0)
    next_t[15] = jnp.int32(15)
    next_t[16] = jnp.int32(15)
    for p in reversed(range(15)):
        nxt = jnp.where(found[p] >= 0, p, nxt)
        next_t[p] = nxt
        slot_t[p] = jnp.maximum(found[p], 0)
    count = jnp.int32(0)
    for p in range(15):
        rank_t[p] = jnp.minimum(count, MOVE - 1)
        count = count + jnp.where(found[p] >= 0, 1, 0)

    def walk_movers(k, p):
        order_t[k] = slot_t[p]
        return next_t[p + 1]

    lax.fori_loop(0, MOVE, walk_movers, next_t[0])

    def back_locals(i, nx):
        s = BLOCKS - 1 - i
        nx = jnp.where(code_t[s] == 0, s, nx)
        local_t[s] = nx
        return nx

    local_t[BLOCKS] = jnp.int32(BLOCKS - 1)
    lax.fori_loop(0, BLOCKS, back_locals, jnp.int32(BLOCKS - 1))

    def number_locals(s, cnt):
        stays = code_t[s] == 0
        sel[s] = jnp.where(stays, jnp.minimum(cnt, STAY - 1), sel[s])
        return cnt + jnp.where(stays, 1, 0)

    lax.fori_loop(0, BLOCKS, number_locals, jnp.int32(0))

    def walk_locals(k, s):
        order_t[MOVE + k] = s
        return local_t[s + 1]

    lax.fori_loop(0, STAY, walk_locals, local_t[0])

    sub = lax.broadcasted_iota(I32, (COLS, COLS), 0)
    lane = lax.broadcasted_iota(I32, (COLS, COLS), 1)
    before = jnp.where(sub < lane, 1.0, 0.0).astype(BF16)
    ones = jnp.full((COLS, COLS), 1.0, BF16)

    def place(s, carry):
        base, table = carry
        o = owner[s]
        row = (o & (NARROW - 1)) * WIDE + (o >> 3)
        member = jnp.where(sub == row, 1.0, 0.0)
        member16 = member.astype(BF16)
        ahead = jnp.dot(member16, before, preferred_element_type=F32) + base
        rank = jnp.sum(ahead * member, axis=0, keepdims=True).astype(I32)
        base = base + jnp.dot(member16, ones, preferred_element_type=F32)
        key[s] = row * 16 + (rank >> 2)
        jrank[s] = rank & 3
        cell = (slot[s] - SLOTS // 2).astype(F32)
        ranked = jnp.where(sub == rank, cell, 0.0).astype(BF16)
        table = table + lax.dot_general(member16, ranked, NT, preferred_element_type=F32)
        return base, table

    zero = jnp.zeros((COLS, COLS), F32)
    _, table = lax.fori_loop(0, BLOCKS, place, (zero, zero))
    sl[...] = table.reshape(NARROW, WIDE, COLS)

    pl.semaphore_wait(barrier, len(wide_peers) + len(narrow_peers))

    slot_narrow = []
    for d in range(1, NARROW):
        p = lax.rem(n + d, NARROW)
        c = pltpu.make_async_remote_copy(
            sl.at[p], s1.at[n], sn_s.at[d], sn_r.at[d], device_id=(w, p), device_id_type=MESH
        )
        c.start()
        slot_narrow.append(c)
    s1[n] = sl[n]

    def big(p, part=None):
        rows = pl.ds(0, DEPTH) if part is None else pl.ds(part * CHUNK, CHUNK)
        return pltpu.make_async_remote_copy(
            send.at[p, rows],
            pool.at[STAY + CODES[p], rows],
            big_s.at[p],
            big_r.at[p],
            device_id=target(p),
            device_id_type=MESH,
        )

    def flux_copy(p):
        return pltpu.make_async_remote_copy(
            fs.at[p], fp.at[STAY + CODES[p]], fl_s.at[p], fl_r.at[p],
            device_id=target(p), device_id_type=MESH,
        )

    def fill(ps):
        for p in ps:
            fs[p] = fm[rank_t[p]]
        for p in ps:
            send[p] = ys[rank_t[p]]

    def send_big(ps):
        for part in range(PARTS):
            for p in ps:
                big(p, part).start()

    def to_pool(q):
        return pltpu.make_async_copy(
            ys.at[pl.ds(GROUP * q, GROUP)],
            pool.at[pl.ds(GROUP * q - MOVE, GROUP)],
            pool_sem.at[q],
        )

    slot_wide = []
    for d in range(1, WIDE):
        q = lax.rem(w + d, WIDE)
        slot_wide.append(
            pltpu.make_async_remote_copy(
                s1t.at[q], s2.at[w], sw_s.at[d], sw_r.at[d], device_id=(q, n), device_id_type=MESH
            )
        )

    for c in loads:
        c.wait()

    @pl.loop(0, BLOCKS // GROUP)
    def _(q):
        x = jnp.concatenate([xs[order_t[GROUP * q + g]] for g in range(GROUP)], axis=1)
        for m in range(DEPTH // CHUNK):
            rows = pl.ds(m * CHUNK, CHUNK)
            hid[rows, :] = silu(
                jnp.dot(w_in[rows, :], x, preferred_element_type=F32)
            ).astype(BF16)
        h = hid[...]
        f = jnp.dot(w_flux[...], h, preferred_element_type=F32)

        @pl.when(q < 2)
        def _():
            for g in range(GROUP):
                fm[GROUP * q + g] = f[:, g * COLS : (g + 1) * COLS]

        @pl.when(q >= 2)
        def _():
            for g in range(GROUP):
                fp[GROUP * q - MOVE + g] = f[:, g * COLS : (g + 1) * COLS]

        for m in range(DEPTH // CHUNK):
            rows = pl.ds(m * CHUNK, CHUNK)
            fresh = jnp.dot(w_out[rows, :], h, preferred_element_type=F32)
            fresh = (fresh + x[m * CHUNK : (m + 1) * CHUNK].astype(F32)).astype(BF16)
            for g in range(GROUP):
                ys[GROUP * q + g, rows] = fresh[:, g * COLS : (g + 1) * COLS]

        @pl.when(q == 0)
        def _():
            fill(range(4))
            for p in range(4):
                flux_copy(p).start()
            send_big(range(4))

        @pl.when(q == 1)
        def _():
            fill(range(4, 15))
            for p in range(4, 15):
                flux_copy(p).start()
            send_big(range(4, EARLY))

        @pl.when(q == 2)
        def _():
            for c in slot_narrow:
                c.wait()
            for p in range(NARROW):
                s1t[:, p, :] = s1[p]
            s2[w] = s1t[w]
            for c in slot_wide:
                c.start()

        @pl.when(q >= 3)
        def _():
            to_pool(q - 1).start()

    for p in range(15):
        flux_copy(p).wait()
    to_pool(BLOCKS // GROUP - 1).start()

    @pl.loop(0, BLOCKS)
    def _(s):
        f = fp[sel[s]] * weight[s]
        j = jrank[s]
        spread = jnp.concatenate([jnp.where(j == k, f, 0.0) for k in range(4)], axis=0)
        bmat[s] = spread.astype(BF16)

    STEP = 512
    row_id = lax.broadcasted_iota(I32, (STEP, COLS), 0)

    @pl.loop(0, 2048 // STEP)
    def _(r):
        acc = jnp.zeros((STEP, COLS), F32)
        for b in range(0, BLOCKS, 4):
            pick = jnp.concatenate(
                [
                    jnp.where(row_id == key[b + g] - r * STEP, 1.0, 0.0).astype(BF16)
                    for g in range(4)
                ],
                axis=1,
            )
            vals = jnp.concatenate([bmat[b + g] for g in range(4)], axis=1)
            acc = acc + lax.dot_general(pick, vals, NT, preferred_element_type=F32)
        msg[pl.ds(2 * r, 2)] = acc.astype(BF16).reshape(2, WIDE, 16, COLS)

    narrow = []
    for d in range(1, NARROW):
        p = lax.rem(n + d, NARROW)
        c = pltpu.make_async_remote_copy(
            msg.at[p], n1.at[:, n], na_s.at[d], na_r.at[d], device_id=(w, p), device_id_type=MESH
        )
        c.start()
        narrow.append(c)
    n1[:, n] = msg[n]
    for c in slot_wide:
        c.wait()
    for c in narrow:
        c.wait()
    wide = []
    for d in range(1, WIDE):
        q = lax.rem(w + d, WIDE)
        c = pltpu.make_async_remote_copy(
            n1.at[q], w2.at[w], wi_s.at[d], wi_r.at[d], device_id=(q, n), device_id_type=MESH
        )
        c.start()
        wide.append(c)
    w2[w] = n1[w]
    send_big(range(EARLY, 15))

    cells = s2[...].reshape(DEVICES, COLS).astype(BF16)
    ROWS = 256
    sub2 = lax.broadcasted_iota(I32, (ROWS, COLS), 0)
    lane2 = lax.broadcasted_iota(I32, (ROWS, COLS), 1)

    @pl.loop(0, 2048 // ROWS)
    def _(r):
        own = jnp.where(lane2 == r * (ROWS // 16) + (sub2 >> 4), 1.0, 0.0).astype(BF16)
        mine = jnp.dot(own, cells, preferred_element_type=F32)
        for j in range(4):
            one = jnp.where(lane2 == 4 * (sub2 & 15) + j, mine, 0.0).astype(BF16)
            cell = jnp.dot(one, ones, preferred_element_type=F32)
            cell = cell.astype(I32) + SLOTS // 2
            for k in range(SLOTS // COLS):
                hot[j, pl.ds(r * ROWS, ROWS), k * COLS : (k + 1) * COLS] = jnp.where(
                    cell == lane2 + k * COLS, 1.0, 0.0
                ).astype(BF16)

    for c in wide:
        c.wait()
    eye = jnp.where(sub == lane, 1.0, 0.0).astype(BF16)
    vals = w2[...].reshape(2048, COLS)
    turned = lax.dot_general(eye, vals, NT, preferred_element_type=F32).astype(BF16)
    total = jnp.zeros((NFLUX, SLOTS), F32)
    for j in range(4):
        total = total + jnp.dot(
            turned[j * NFLUX : (j + 1) * NFLUX], hot[j], preferred_element_type=F32
        )
    ocean[...] = total

    for q in range(2, BLOCKS // GROUP):
        to_pool(q).wait()
    for p in range(15):
        big(p).wait()


def final_kernel(sel, pool, out, buf, in_sem, out_sem):
    def fetch(s):
        return pltpu.make_async_copy(pool.at[sel[s]], buf.at[s], in_sem.at[s])

    def put(s):
        return pltpu.make_async_copy(buf.at[s], out.at[s], out_sem.at[s])

    for s in range(BLOCKS):
        fetch(s).start()
    for s in range(BLOCKS):
        fetch(s).wait()
        put(s).start()
    for s in range(BLOCKS):
        put(s).wait()


def per_device(state, group_of, w_in, w_out, w_flux, owner, ocean_slot, remap_weight):
    vmem, anys, smem = (
        pl.BlockSpec(memory_space=pltpu.VMEM),
        pl.BlockSpec(memory_space=pl.ANY),
        pl.BlockSpec(memory_space=pltpu.SMEM),
    )
    dma = pltpu.SemaphoreType.DMA
    pool, ocean, sel = pl.pallas_call(
        main_kernel,
        out_shape=(
            jax.ShapeDtypeStruct((STAY + WIDE, DEPTH, COLS), BF16),
            jax.ShapeDtypeStruct((NFLUX, SLOTS), F32),
            jax.ShapeDtypeStruct((BLOCKS,), I32),
        ),
        in_specs=[smem, anys, anys, anys, vmem, vmem, vmem, vmem],
        out_specs=(anys, vmem, smem),
        scratch_shapes=[
            pltpu.VMEM((BLOCKS, DEPTH, COLS), BF16),
            pltpu.VMEM((BLOCKS, DEPTH, COLS), BF16),
            pltpu.VMEM((15, DEPTH, COLS), BF16),
            pltpu.VMEM((DEPTH, DEPTH), BF16),
            pltpu.VMEM((DEPTH, DEPTH), BF16),
            pltpu.VMEM((DEPTH, GROUP * COLS), BF16),
            pltpu.VMEM((MOVE, NFLUX, COLS), F32),
            pltpu.VMEM((15, NFLUX, COLS), F32),
            pltpu.VMEM((STAY + WIDE, NFLUX, COLS), F32),
            pltpu.VMEM((BLOCKS, 1, COLS), I32),
            pltpu.VMEM((BLOCKS, 1, COLS), I32),
            pltpu.VMEM((BLOCKS, COLS, COLS), BF16),
            pltpu.VMEM((NARROW, WIDE, 16, COLS), BF16),
            pltpu.VMEM((WIDE, NARROW, 16, COLS), BF16),
            pltpu.VMEM((WIDE, NARROW, 16, COLS), BF16),
            pltpu.VMEM((NARROW, WIDE, COLS), F32),
            pltpu.VMEM((NARROW, WIDE, COLS), F32),
            pltpu.VMEM((WIDE, NARROW, COLS), F32),
            pltpu.VMEM((WIDE, NARROW, COLS), F32),
            pltpu.VMEM((4, 2048, SLOTS), BF16),
            pltpu.SMEM((BLOCKS,), I32),
            pltpu.SMEM((16,), I32),
            pltpu.SMEM((17,), I32),
            pltpu.SMEM((15,), I32),
            pltpu.SMEM((BLOCKS,), I32),
            pltpu.SMEM((BLOCKS + 1,), I32),
            dma((10,)),
            dma((8,)),
            dma((15,)),
            dma((15,)),
            dma((15,)),
            dma((15,)),
            dma((NARROW,)),
            dma((NARROW,)),
            dma((WIDE,)),
            dma((WIDE,)),
            dma((NARROW,)),
            dma((NARROW,)),
            dma((WIDE,)),
            dma((WIDE,)),
        ],
        compiler_params=pltpu.CompilerParams(
            collective_id=1, has_side_effects=True, vmem_limit_bytes=60 * 2**20
        ),
        name="physics",
    )(
        group_of,
        state,
        w_in,
        w_out,
        w_flux,
        owner.reshape(BLOCKS, 1, COLS),
        ocean_slot.reshape(BLOCKS, 1, COLS),
        remap_weight.reshape(BLOCKS, 1, COLS),
    )
    new_state = pl.pallas_call(
        final_kernel,
        out_shape=jax.ShapeDtypeStruct((BLOCKS, DEPTH, COLS), BF16),
        in_specs=[smem, anys],
        out_specs=anys,
        scratch_shapes=[
            pltpu.VMEM((BLOCKS, DEPTH, COLS), BF16),
            dma((BLOCKS,)),
            dma((BLOCKS,)),
        ],
        name="assemble",
    )(sel, pool)
    return new_state, ocean


def solution(mesh):
    rows = P(("wide", "narrow"))
    in_specs = (P(("wide", "narrow"), None, None), P(), P(), P(), P(), P(("wide", "narrow"), None), rows, rows)
    out_specs = (P(("wide", "narrow"), None, None), P(None, ("wide", "narrow")))
    return jax.shard_map(
        per_device, mesh=mesh, in_specs=in_specs, out_specs=out_specs, check_vma=False
    )
```

```python
import functools

import jax
import jax.numpy as jnp
from jax import lax
from jax.experimental import pallas as pl
from jax.experimental.pallas import tpu as pltpu
from jax.sharding import PartitionSpec as P

F32, BF16, I32 = jnp.float32, jnp.bfloat16, jnp.int32
MESH = pl.DeviceIdType.MESH
NT = (((1,), (1,)), ((), ()))

BLOCKS, DEPTH, COLS = 32, 1024, 128
NFLUX, SLOTS = 32, 512
WIDE, NARROW, SIDE = 16, 8, 4
DEVICES = WIDE * NARROW
MOVE, STAY = 8, 24
GROUP = 4
CHUNK = 256
ITEMS = (
    (1, 0), (3, 0), (0, 1), (0, 3), (2, 2), (1, 1), (3, 3), (1, 3),
    (3, 1), (2, 1), (2, 3), (1, 2), (3, 2), (2, 0), (0, 2),
)
CODES = tuple(dz * SIDE + dy for dy, dz in ITEMS)
PARTS = 4
ORDER = [(p, part) for part in range(PARTS) for p in range(4)]
ORDER += [(p, part) for part in range(PARTS) for p in range(4, 15)]
SENT = (16, 24, 28, 32, 36, 40, 44, 48)
SENT_SORT = 52
SENT_NARROW = 56


def silu(v):
    return v / (1.0 + jnp.exp(-v))


def main_kernel(
    group_of, state, w_in_hbm, w_out_hbm, w_flux, owner, slot, weight,
    pool, ocean, sel,
    xs, ys, send, w_in, w_out, hid, fm, fs, fp, fr, key, jrank, bmat, msg, n1, w2, sl, s1, s1t, s2, hot,
    code_t, slot_t, next_t, rank_t, order_t, local_t,
    load_sem, big_s, big_r, fl_s, fl_r, na_s, na_r, wi_s, wi_r, sn_s, sn_r, sw_s, sw_r,
):
    w, n = lax.axis_index("wide"), lax.axis_index("narrow")
    y, z = lax.rem(w, SIDE), lax.div(w, SIDE)
    loads = [
        pltpu.make_async_copy(w_in_hbm, w_in, load_sem.at[0]),
        pltpu.make_async_copy(w_out_hbm, w_out, load_sem.at[9]),
    ]
    for i in range(8):
        loads.append(
            pltpu.make_async_copy(
                state.at[pl.ds(4 * i, 4)], xs.at[pl.ds(4 * i, 4)], load_sem.at[1 + i]
            )
        )
    loads[0].start()
    for c in loads[2:]:
        c.start()
    loads[1].start()

    def target(p):
        dy, dz = ITEMS[p]
        return (lax.rem(z + dz, SIDE) * SIDE + lax.rem(y + dy, SIDE), n)

    wide_peers = [(lax.rem(w + d, WIDE), n) for d in range(1, WIDE)]
    narrow_peers = [(w, lax.rem(n + d, NARROW)) for d in range(1, NARROW)]
    barrier = pltpu.get_barrier_semaphore()
    for peer in wide_peers + narrow_peers:
        pl.semaphore_signal(barrier, inc=1, device_id=peer, device_id_type=MESH)

    base_row = (w * NARROW + n) * BLOCKS

    def scan_slots(s, found):
        t = lax.div(group_of[base_row + s], NARROW * BLOCKS)
        dy = lax.rem(lax.rem(t, SIDE) - y + SIDE, SIDE)
        dz = lax.rem(lax.div(t, SIDE) - z + SIDE, SIDE)
        src = lax.rem(2 * w - t + 2 * WIDE, WIDE)
        ry = lax.rem(y - lax.rem(src, SIDE) + SIDE, SIDE)
        rz = lax.rem(z - lax.div(src, SIDE) + SIDE, SIDE)
        code = dz * SIDE + dy
        code_t[s] = code
        sel[s] = STAY + rz * SIDE + ry
        return tuple(jnp.where(code == CODES[p], s, found[p]) for p in range(15))

    found = lax.fori_loop(0, BLOCKS, scan_slots, (jnp.int32(-1),) * 15)
    nxt = jnp.int32(15)
    slot_t[15] = jnp.int32(0)
    next_t[15] = jnp.int32(15)
    next_t[16] = jnp.int32(15)
    for p in reversed(range(15)):
        nxt = jnp.where(found[p] >= 0, p, nxt)
        next_t[p] = nxt
        slot_t[p] = jnp.maximum(found[p], 0)
    count = jnp.int32(0)
    for p in range(15):
        rank_t[p] = jnp.minimum(count, MOVE - 1)
        count = count + jnp.where(found[p] >= 0, 1, 0)

    def walk_movers(k, p):
        order_t[k] = slot_t[p]
        return next_t[p + 1]

    lax.fori_loop(0, MOVE, walk_movers, next_t[0])

    def back_locals(i, nx):
        s = BLOCKS - 1 - i
        nx = jnp.where(code_t[s] == 0, s, nx)
        local_t[s] = nx
        return nx

    local_t[BLOCKS] = jnp.int32(BLOCKS - 1)
    lax.fori_loop(0, BLOCKS, back_locals, jnp.int32(BLOCKS - 1))

    def number_locals(s, cnt):
        stays = code_t[s] == 0
        sel[s] = jnp.where(stays, jnp.minimum(cnt, STAY - 1), sel[s])
        return cnt + jnp.where(stays, 1, 0)

    lax.fori_loop(0, BLOCKS, number_locals, jnp.int32(0))

    def walk_locals(k, s):
        order_t[MOVE + k] = s
        return local_t[s + 1]

    lax.fori_loop(0, STAY, walk_locals, local_t[0])

    sub = lax.broadcasted_iota(I32, (COLS, COLS), 0)
    lane = lax.broadcasted_iota(I32, (COLS, COLS), 1)
    before = jnp.where(sub < lane, 1.0, 0.0).astype(BF16)
    ones = jnp.full((COLS, COLS), 1.0, BF16)

    def place(i, carry):
        base, table = carry
        for g in range(4):
            s = 4 * i + g
            o = owner[s]
            row = (o & (NARROW - 1)) * WIDE + (o >> 3)
            member = jnp.where(sub == row, 1.0, 0.0)
            member16 = member.astype(BF16)
            ahead = jnp.dot(member16, before, preferred_element_type=F32)
            count = jnp.dot(member16, ones, preferred_element_type=F32)
            rank = jnp.sum((ahead + base) * member, axis=0, keepdims=True).astype(I32)
            base = base + count
            key[s] = row * 16 + (rank >> 2)
            jrank[s] = rank & 3
            cell = (slot[s] - SLOTS // 2).astype(F32)
            ranked = jnp.where(sub == rank, cell, 0.0).astype(BF16)
            table = table + lax.dot_general(member16, ranked, NT, preferred_element_type=F32)
        return base, table

    def slots_out():
        zero = jnp.zeros((COLS, COLS), F32)
        _, table = lax.fori_loop(0, BLOCKS // 4, place, (zero, zero))
        sl[...] = table.reshape(NARROW, WIDE, COLS)
        for c in slot_narrow:
            c.start()
        s1[n] = sl[n]


    slot_narrow = []
    for d in range(1, NARROW):
        p = lax.rem(n + d, NARROW)
        c = pltpu.make_async_remote_copy(
            sl.at[p], s1.at[n], sn_s.at[d], sn_r.at[d], device_id=(w, p), device_id_type=MESH
        )
        slot_narrow.append(c)

    def big(p, part=None):
        rows = pl.ds(0, DEPTH) if part is None else pl.ds(part * CHUNK, CHUNK)
        return pltpu.make_async_remote_copy(
            send.at[p, rows],
            pool.at[STAY + CODES[p], rows],
            big_s.at[p],
            big_r.at[p],
            device_id=target(p),
            device_id_type=MESH,
        )

    def flux_copy(p):
        return pltpu.make_async_remote_copy(
            fs.at[p], fr.at[CODES[p]], fl_s.at[p], fl_r.at[p],
            device_id=target(p), device_id_type=MESH,
        )

    def fill(ps):
        for p in ps:
            fs[p] = fm[rank_t[p]].astype(BF16)
        for p in ps:
            send[p] = ys[rank_t[p]]

    def send_big(first, last):
        for p, part in ORDER[first:last]:
            big(p, part).start()

    slot_wide = []
    for d in range(1, WIDE):
        q = lax.rem(w + d, WIDE)
        slot_wide.append(
            pltpu.make_async_remote_copy(
                s1t.at[q], s2.at[w], sw_s.at[d], sw_r.at[d], device_id=(q, n), device_id_type=MESH
            )
        )

    for c in loads:
        c.wait()

    @pl.loop(0, BLOCKS // GROUP)
    def _(q):
        x = jnp.concatenate([xs[order_t[GROUP * q + g]] for g in range(GROUP)], axis=1)
        for m in range(DEPTH // CHUNK):
            rows = pl.ds(m * CHUNK, CHUNK)
            hid[rows, :] = silu(
                jnp.dot(w_in[rows, :], x, preferred_element_type=F32)
            ).astype(BF16)
        h = hid[...]
        f = jnp.dot(w_flux[...], h, preferred_element_type=F32)

        @pl.when(q < 2)
        def _():
            for g in range(GROUP):
                fm[GROUP * q + g] = f[:, g * COLS : (g + 1) * COLS]

        @pl.when(q >= 2)
        def _():
            for g in range(GROUP):
                fp[GROUP * q - MOVE + g] = f[:, g * COLS : (g + 1) * COLS]

        for m in range(DEPTH // CHUNK):
            rows = pl.ds(m * CHUNK, CHUNK)
            fresh = jnp.dot(w_out[rows, :], h, preferred_element_type=F32)
            fresh = (fresh + x[m * CHUNK : (m + 1) * CHUNK].astype(F32)).astype(BF16)

            @pl.when(q < 2)
            def _(rows=rows, fresh=fresh):
                for g in range(GROUP):
                    ys[GROUP * q + g, rows] = fresh[:, g * COLS : (g + 1) * COLS]

            @pl.when(q >= 2)
            def _(rows=rows, fresh=fresh):
                for g in range(GROUP):
                    pool[GROUP * q - MOVE + g, rows] = fresh[:, g * COLS : (g + 1) * COLS]

        @pl.when(q == 0)
        def _():
            fill(range(4))
            pl.semaphore_wait(barrier, len(wide_peers) + len(narrow_peers))
            for p in range(4):
                flux_copy(p).start()
            send_big(0, SENT[0])

        @pl.when(q == 1)
        def _():
            fill(range(4, 15))
            for p in range(4, 15):
                flux_copy(p).start()
            send_big(SENT[0], SENT[1])
            slots_out()

        @pl.when(q == 3)
        def _():
            for c in slot_narrow:
                c.wait()
            for p in range(NARROW):
                s1t[:, p, :] = s1[p]
            s2[w] = s1t[w]
            for c in slot_wide:
                c.start()

        for step in range(2, BLOCKS // GROUP):

            @pl.when(q == step)
            def _(step=step):
                send_big(SENT[step - 1], SENT[step])


    for p in range(15):
        flux_copy(p).wait()
    fp[STAY:] = fr[...].astype(F32)

    send_big(SENT[-1], SENT_SORT)

    @pl.loop(0, BLOCKS)
    def _(s):
        f = fp[sel[s]] * weight[s]
        j = jrank[s]
        spread = jnp.concatenate([jnp.where(j == k, f, 0.0) for k in range(4)], axis=0)
        bmat[s] = spread.astype(BF16)

    HALF = WIDE * 16
    row_id = lax.broadcasted_iota(I32, (2 * HALF, COLS), 0)

    def narrow_copy(d):
        p = lax.rem(n + d, NARROW)
        return pltpu.make_async_remote_copy(
            msg.at[p], n1.at[:, n], na_s.at[d], na_r.at[d], device_id=(w, p), device_id_type=MESH
        )

    @pl.loop(0, NARROW // 2)
    def _(r):
        d = 2 * r + 1
        p0, p1 = lax.rem(n + d, NARROW), lax.rem(n + d + 1, NARROW)
        wanted = row_id + jnp.where(row_id < HALF, p0 * HALF, (p1 - 1) * HALF)
        acc = jnp.zeros((2 * HALF, COLS), F32)
        for b in range(0, BLOCKS, 4):
            pick = jnp.concatenate(
                [jnp.where(wanted == key[b + g], 1.0, 0.0).astype(BF16) for g in range(4)],
                axis=1,
            )
            vals = jnp.concatenate([bmat[b + g] for g in range(4)], axis=1)
            acc = acc + lax.dot_general(pick, vals, NT, preferred_element_type=F32)
        both = acc.astype(BF16).reshape(2, WIDE, 16, COLS)
        msg[p0] = both[0]
        msg[p1] = both[1]
        narrow_copy(d).start()

        @pl.when(r < NARROW // 2 - 1)
        def _():
            narrow_copy(d + 1).start()

    send_big(SENT_SORT, SENT_NARROW)
    n1[:, n] = msg[n]
    for c in slot_wide:
        c.wait()
    for d in range(1, NARROW):
        narrow_copy(d).wait()
    wide = []
    for d in range(1, WIDE):
        q = lax.rem(w + d, WIDE)
        c = pltpu.make_async_remote_copy(
            n1.at[q], w2.at[w], wi_s.at[d], wi_r.at[d], device_id=(q, n), device_id_type=MESH
        )
        c.start()
        wide.append(c)
    w2[w] = n1[w]
    send_big(SENT_NARROW, len(ORDER))

    cells = s2[...].reshape(DEVICES, COLS).astype(BF16)
    ROWS = 256
    sub2 = lax.broadcasted_iota(I32, (ROWS, COLS), 0)
    lane2 = lax.broadcasted_iota(I32, (ROWS, COLS), 1)

    @pl.loop(0, 2048 // ROWS)
    def _(r):
        own = jnp.where(lane2 == r * (ROWS // 16) + (sub2 >> 4), 1.0, 0.0).astype(BF16)
        mine = jnp.dot(own, cells, preferred_element_type=F32)
        for j in range(4):
            one = jnp.where(lane2 == 4 * (sub2 & 15) + j, mine, 0.0).astype(BF16)
            cell = jnp.dot(one, ones, preferred_element_type=F32)
            cell = cell.astype(I32) + SLOTS // 2
            for k in range(SLOTS // COLS):
                hot[j, pl.ds(r * ROWS, ROWS), k * COLS : (k + 1) * COLS] = jnp.where(
                    cell == lane2 + k * COLS, 1.0, 0.0
                ).astype(BF16)

    for c in wide:
        c.wait()
    eye = jnp.where(sub == lane, 1.0, 0.0).astype(BF16)
    vals = w2[...].reshape(2048, COLS)
    turned = lax.dot_general(eye, vals, NT, preferred_element_type=F32).astype(BF16)
    total = jnp.zeros((NFLUX, SLOTS), F32)
    for j in range(4):
        total = total + jnp.dot(
            turned[j * NFLUX : (j + 1) * NFLUX], hot[j], preferred_element_type=F32
        )
    ocean[...] = total

    for p in range(15):
        big(p).wait()


def final_kernel(sel, pool, cells, out, ocean, sem, cell_sem):
    def put(s):
        return pltpu.make_async_copy(pool.at[sel[s]], out.at[s], sem.at[s])

    for s in range(BLOCKS):
        put(s).start()
    last = pltpu.make_async_copy(cells, ocean, cell_sem)
    last.start()
    for s in range(BLOCKS):
        put(s).wait()
    last.wait()


def per_device(state, group_of, w_in, w_out, w_flux, owner, ocean_slot, remap_weight):
    vmem, hbm, smem = (
        pl.BlockSpec(memory_space=pltpu.VMEM),
        pl.BlockSpec(memory_space=pltpu.HBM),
        pl.BlockSpec(memory_space=pltpu.SMEM),
    )
    dma = pltpu.SemaphoreType.DMA
    pool, ocean, sel = pl.pallas_call(
        main_kernel,
        out_shape=(
            pltpu.VMEM((STAY + WIDE, DEPTH, COLS), BF16),
            jax.ShapeDtypeStruct((NFLUX, SLOTS), F32),
            jax.ShapeDtypeStruct((BLOCKS,), I32),
        ),
        in_specs=[smem, hbm, hbm, hbm, vmem, vmem, vmem, vmem],
        out_specs=(vmem, vmem, smem),
        scratch_shapes=[
            pltpu.VMEM((BLOCKS, DEPTH, COLS), BF16),
            pltpu.VMEM((MOVE, DEPTH, COLS), BF16),
            pltpu.VMEM((15, DEPTH, COLS), BF16),
            pltpu.VMEM((DEPTH, DEPTH), BF16),
            pltpu.VMEM((DEPTH, DEPTH), BF16),
            pltpu.VMEM((DEPTH, GROUP * COLS), BF16),
            pltpu.VMEM((MOVE, NFLUX, COLS), F32),
            pltpu.VMEM((15, NFLUX, COLS), BF16),
            pltpu.VMEM((STAY + WIDE, NFLUX, COLS), F32),
            pltpu.VMEM((WIDE, NFLUX, COLS), BF16),
            pltpu.VMEM((BLOCKS, 1, COLS), I32),
            pltpu.VMEM((BLOCKS, 1, COLS), I32),
            pltpu.VMEM((BLOCKS, COLS, COLS), BF16),
            pltpu.VMEM((NARROW, WIDE, 16, COLS), BF16),
            pltpu.VMEM((WIDE, NARROW, 16, COLS), BF16),
            pltpu.VMEM((WIDE, NARROW, 16, COLS), BF16),
            pltpu.VMEM((NARROW, WIDE, COLS), F32),
            pltpu.VMEM((NARROW, WIDE, COLS), F32),
            pltpu.VMEM((WIDE, NARROW, COLS), F32),
            pltpu.VMEM((WIDE, NARROW, COLS), F32),
            pltpu.VMEM((4, 2048, SLOTS), BF16),
            pltpu.SMEM((BLOCKS,), I32),
            pltpu.SMEM((16,), I32),
            pltpu.SMEM((17,), I32),
            pltpu.SMEM((15,), I32),
            pltpu.SMEM((BLOCKS,), I32),
            pltpu.SMEM((BLOCKS + 1,), I32),
            dma((10,)),
            dma((15,)),
            dma((15,)),
            dma((15,)),
            dma((15,)),
            dma((NARROW,)),
            dma((NARROW,)),
            dma((WIDE,)),
            dma((WIDE,)),
            dma((NARROW,)),
            dma((NARROW,)),
            dma((WIDE,)),
            dma((WIDE,)),
        ],
        compiler_params=pltpu.CompilerParams(
            collective_id=1, has_side_effects=True, vmem_limit_bytes=49 * 2**20
        ),
        name="physics",
    )(
        group_of,
        state,
        w_in,
        w_out,
        w_flux,
        owner.reshape(BLOCKS, 1, COLS),
        ocean_slot.reshape(BLOCKS, 1, COLS),
        remap_weight.reshape(BLOCKS, 1, COLS),
    )
    return pl.pallas_call(
        final_kernel,
        out_shape=(
            jax.ShapeDtypeStruct((BLOCKS, DEPTH, COLS), BF16),
            jax.ShapeDtypeStruct((NFLUX, SLOTS), F32),
        ),
        in_specs=[smem, vmem, vmem],
        out_specs=(hbm, hbm),
        scratch_shapes=[dma((BLOCKS,)), dma],
        compiler_params=pltpu.CompilerParams(vmem_limit_bytes=2 * 2**20),
        name="assemble",
    )(sel, pool, ocean)


def solution(mesh):
    rows = P(("wide", "narrow"))
    in_specs = (P(("wide", "narrow"), None, None), P(), P(), P(), P(), P(("wide", "narrow"), None), rows, rows)
    out_specs = (P(("wide", "narrow"), None, None), P(None, ("wide", "narrow")))
    return jax.shard_map(
        per_device, mesh=mesh, in_specs=in_specs, out_specs=out_specs, check_vma=False
    )
```

```python
import functools

import jax
import jax.numpy as jnp
from jax import lax
from jax.experimental import pallas as pl
from jax.experimental.pallas import tpu as pltpu
from jax.sharding import PartitionSpec as P

F32, BF16, I32 = jnp.float32, jnp.bfloat16, jnp.int32
MESH = pl.DeviceIdType.MESH
NT = (((1,), (1,)), ((), ()))

BLOCKS, DEPTH, COLS = 32, 1024, 128
NFLUX, SLOTS = 32, 512
WIDE, NARROW, SIDE = 16, 8, 4
DEVICES = WIDE * NARROW
MOVE, STAY = 8, 24
GROUP = 4
CHUNK = 256
ITEMS = (
    (1, 0), (3, 0), (0, 1), (0, 3), (1, 1), (3, 3), (1, 3), (3, 1),
    (2, 2), (2, 1), (2, 3), (1, 2), (3, 2), (2, 0), (0, 2),
)
CODES = tuple(dz * SIDE + dy for dy, dz in ITEMS)
RAW = 4
PARTS = 4
ORDER = [(p, part) for part in range(PARTS) for p in range(4, 8)]
ORDER += [(p, part) for part in range(PARTS) for p in range(8, 15)]
SENT = (16, 22, 25, 28, 31, 34, 36, 38)
SENT_LAST = 39
SENT_SORT = 40
SENT_NARROW = 42


def silu(v):
    return v / (1.0 + jnp.exp(-v))


def main_kernel(
    group_of, state, w_in_hbm, w_out_hbm, w_flux_hbm, owner, slot, weight,
    pool, ocean, sel,
    xs, rx, ys, send, w_in, w_out, hid, fm, fs, fp, fr, key, jrank, bmat, msg, n1, w2, ahead_of, cells_of, sl, s1, s1t, s2, hot,
    code_t, slot_t, next_t, rank_t, order_t, local_t,
    load_sem, big_s, big_r, fl_s, fl_r, na_s, na_r, wi_s, wi_r, sn_s, sn_r, sw_s, sw_r,
):
    w, n = lax.axis_index("wide"), lax.axis_index("narrow")
    y, z = lax.rem(w, SIDE), lax.div(w, SIDE)
    loads = [
        pltpu.make_async_copy(w_in_hbm, w_in, load_sem.at[0]),
        pltpu.make_async_copy(w_out_hbm, w_out.at[pl.ds(0, DEPTH)], load_sem.at[9]),
        pltpu.make_async_copy(w_flux_hbm, w_out.at[pl.ds(DEPTH, NFLUX)], load_sem.at[10]),
    ]
    for i in range(8):
        loads.append(
            pltpu.make_async_copy(
                state.at[pl.ds(4 * i, 4)], xs.at[pl.ds(4 * i, 4)], load_sem.at[1 + i]
            )
        )
    for c in loads[3:]:
        c.start()
    for c in loads[:3]:
        c.start()

    def target(p):
        dy, dz = ITEMS[p]
        return (lax.rem(z + dz, SIDE) * SIDE + lax.rem(y + dy, SIDE), n)

    wide_peers = [(lax.rem(w + d, WIDE), n) for d in range(1, WIDE)]
    narrow_peers = [(w, lax.rem(n + d, NARROW)) for d in range(1, NARROW)]
    barrier = pltpu.get_barrier_semaphore()
    for peer in wide_peers + narrow_peers:
        pl.semaphore_signal(barrier, inc=1, device_id=peer, device_id_type=MESH)

    base_row = (w * NARROW + n) * BLOCKS

    def scan_slots(s, found):
        t = lax.div(group_of[base_row + s], NARROW * BLOCKS)
        dy = lax.rem(lax.rem(t, SIDE) - y + SIDE, SIDE)
        dz = lax.rem(lax.div(t, SIDE) - z + SIDE, SIDE)
        src = lax.rem(2 * w - t + 2 * WIDE, WIDE)
        ry = lax.rem(y - lax.rem(src, SIDE) + SIDE, SIDE)
        rz = lax.rem(z - lax.div(src, SIDE) + SIDE, SIDE)
        code = dz * SIDE + dy
        code_t[s] = code
        sel[s] = STAY + rz * SIDE + ry
        return tuple(jnp.where(code == CODES[p], s, found[p]) for p in range(15))

    found = lax.fori_loop(0, BLOCKS, scan_slots, (jnp.int32(-1),) * 15)
    nxt = jnp.int32(15)
    slot_t[15] = jnp.int32(0)
    next_t[15] = jnp.int32(15)
    next_t[16] = jnp.int32(15)
    for p in reversed(range(15)):
        nxt = jnp.where(found[p] >= 0, p, nxt)
        next_t[p] = nxt
        slot_t[p] = jnp.maximum(found[p], 0)
    count = jnp.int32(0)
    for p in range(RAW, 15):
        rank_t[p] = jnp.minimum(count, MOVE - 1)
        count = count + jnp.where(found[p] >= 0, 1, 0)

    def walk_movers(k, p):
        order_t[k] = slot_t[p]
        return next_t[p + 1]

    lax.fori_loop(0, MOVE, walk_movers, next_t[RAW])

    def back_locals(i, nx):
        s = BLOCKS - 1 - i
        nx = jnp.where(code_t[s] == 0, s, nx)
        local_t[s] = nx
        return nx

    local_t[BLOCKS] = jnp.int32(BLOCKS - 1)
    lax.fori_loop(0, BLOCKS, back_locals, jnp.int32(BLOCKS - 1))

    def number_locals(s, cnt):
        stays = code_t[s] == 0
        sel[s] = jnp.where(stays, jnp.minimum(cnt, STAY - 1), sel[s])
        return cnt + jnp.where(stays, 1, 0)

    lax.fori_loop(0, BLOCKS, number_locals, jnp.int32(0))

    def walk_locals(k, s):
        order_t[MOVE + k] = s
        return local_t[s + 1]

    lax.fori_loop(0, STAY, walk_locals, local_t[0])

    sub = lax.broadcasted_iota(I32, (COLS, COLS), 0)
    lane = lax.broadcasted_iota(I32, (COLS, COLS), 1)
    before = jnp.where(sub < lane, 1.0, 0.0).astype(BF16)
    ones = jnp.full((COLS, COLS), 1.0, BF16)

    ahead_of[...] = jnp.zeros((COLS, COLS), F32)
    cells_of[...] = jnp.zeros((COLS, COLS), F32)

    def place(i):
        base, table = ahead_of[...], cells_of[...]
        for g in range(4):
            s = 4 * i + g
            o = owner[s]
            row = (o & (NARROW - 1)) * WIDE + (o >> 3)
            member = jnp.where(sub == row, 1.0, 0.0)
            member16 = member.astype(BF16)
            ahead = jnp.dot(member16, before, preferred_element_type=F32)
            count = jnp.dot(member16, ones, preferred_element_type=F32)
            rank = jnp.sum((ahead + base) * member, axis=0, keepdims=True).astype(I32)
            base = base + count
            key[s] = row * 8 + (rank >> 3)
            jrank[s] = rank & 7
            cell = (slot[s] - SLOTS // 2).astype(F32)
            ranked = jnp.where(sub == rank, cell, 0.0).astype(BF16)
            table = table + lax.dot_general(member16, ranked, NT, preferred_element_type=F32)
        ahead_of[...] = base
        cells_of[...] = table

    def slots_out():
        sl[...] = cells_of[...].reshape(NARROW, WIDE, COLS)
        for c in slot_narrow:
            c.start()
        s1[n] = sl[n]

    slot_narrow = []
    for d in range(1, NARROW):
        p = lax.rem(n + d, NARROW)
        c = pltpu.make_async_remote_copy(
            sl.at[p], s1.at[n], sn_s.at[d], sn_r.at[d], device_id=(w, p), device_id_type=MESH
        )
        slot_narrow.append(c)

    def big(p, part=None):
        rows = pl.ds(0, DEPTH) if part is None else pl.ds(part * CHUNK, CHUNK)
        return pltpu.make_async_remote_copy(
            send.at[p, rows],
            rx.at[p, rows] if p < RAW else pool.at[STAY + CODES[p], rows],
            big_s.at[p],
            big_r.at[p],
            device_id=target(p),
            device_id_type=MESH,
        )

    def flux_copy(p):
        return pltpu.make_async_remote_copy(
            fs.at[p], fr.at[CODES[p]], fl_s.at[p], fl_r.at[p],
            device_id=target(p), device_id_type=MESH,
        )

    def fill(ps):
        for p in ps:
            fs[p] = fm[rank_t[p]].astype(BF16)
        for p in ps:
            send[p] = ys[rank_t[p]]

    def send_big(first, last):
        for p, part in ORDER[first:last]:
            big(p, part).start()

    slot_wide = []
    for d in range(1, WIDE):
        q = lax.rem(w + d, WIDE)
        slot_wide.append(
            pltpu.make_async_remote_copy(
                s1t.at[q], s2.at[w], sw_s.at[d], sw_r.at[d], device_id=(q, n), device_id_type=MESH
            )
        )

    for c in loads[3:]:
        c.wait()
    for p in range(RAW):
        send[p] = xs[slot_t[p]]
    pl.semaphore_wait(barrier, len(wide_peers) + len(narrow_peers))
    for part in range(PARTS):
        for p in range(RAW):
            big(p, part).start()
    for c in loads[:3]:
        c.wait()

    def columns(v, g):
        return v[:, g * COLS : (g + 1) * COLS]

    def compute(x, put_flux, put_rows):
        for m in range(DEPTH // CHUNK):
            rows = pl.ds(m * CHUNK, CHUNK)
            hid[rows, :] = silu(
                jnp.dot(w_in[rows, :], x, preferred_element_type=F32)
            ).astype(BF16)
        h = hid[...]
        for m in range(DEPTH // CHUNK):
            last = m == DEPTH // CHUNK - 1
            rows = pl.ds(m * CHUNK, CHUNK)
            both = jnp.dot(
                w_out[pl.ds(m * CHUNK, CHUNK + (NFLUX if last else 0)), :],
                h,
                preferred_element_type=F32,
            )
            fresh = both[:CHUNK] + x[m * CHUNK : (m + 1) * CHUNK].astype(F32)
            put_rows(rows, fresh.astype(BF16))
            if last:
                put_flux(both[CHUNK:])

    def gathered(q):
        return jnp.concatenate([xs[order_t[GROUP * q + g]] for g in range(GROUP)], axis=1)

    def moved(q):
        def put_flux(f):
            for g in range(GROUP):
                fm[GROUP * q + g] = columns(f, g)

        def put_rows(rows, fresh):
            for g in range(GROUP):
                ys[GROUP * q + g, rows] = columns(fresh, g)

        place(q)
        compute(gathered(q), put_flux, put_rows)

    def send_moved(ps, first, last):
        fill(ps)
        for p in ps:
            flux_copy(p).start()
        send_big(first, last)

    moved(0)
    send_moved(range(4, 8), 0, SENT[0])
    moved(1)
    send_moved(range(8, 15), SENT[0], SENT[1])

    @pl.loop(0, STAY // GROUP)
    def _(k):
        def put_flux(f):
            for g in range(GROUP):
                fp[GROUP * k + g] = columns(f, g)

        def put_rows(rows, fresh):
            for g in range(GROUP):
                pool[GROUP * k + g, rows] = columns(fresh, g)

        place(k + 2)
        compute(gathered(k + 2), put_flux, put_rows)
        for step in range(STAY // GROUP):

            @pl.when(k == step)
            def _(step=step):
                send_big(SENT[step + 1], SENT[step + 2])

    slots_out()

    for p in range(RAW):
        big(p).wait_recv()

    def raw_flux(f):
        for p in range(RAW):
            fp[STAY + CODES[p]] = columns(f, p)

    def raw_rows(rows, fresh):
        for p in range(RAW):
            pool[STAY + CODES[p], rows] = columns(fresh, p)

    compute(jnp.concatenate([rx[p] for p in range(RAW)], axis=1), raw_flux, raw_rows)

    for c in slot_narrow:
        c.wait()
    for p in range(NARROW):
        s1t[:, p, :] = s1[p]
    s2[w] = s1t[w]
    for c in slot_wide:
        c.start()
    send_big(SENT[-1], SENT_LAST)

    for p in range(RAW, 15):
        flux_copy(p).wait()
        fp[STAY + CODES[p]] = fr[CODES[p]].astype(F32)
    send_big(SENT_LAST, SENT_SORT)

    @pl.loop(0, BLOCKS)
    def _(s):
        f = fp[sel[s]] * weight[s]
        j = jrank[s]
        spread = jnp.concatenate([jnp.where(j == k, f, 0.0) for k in range(8)], axis=0)
        bmat[s] = spread.astype(BF16)

    HALF = WIDE * 8
    row_id = lax.broadcasted_iota(I32, (2 * HALF, COLS), 0)

    def narrow_copy(d):
        p = lax.rem(n + d, NARROW)
        return pltpu.make_async_remote_copy(
            msg.at[p], n1.at[:, n], na_s.at[d], na_r.at[d], device_id=(w, p), device_id_type=MESH
        )

    @pl.loop(0, NARROW // 2)
    def _(r):
        d = 2 * r + 1
        p0, p1 = lax.rem(n + d, NARROW), lax.rem(n + d + 1, NARROW)
        wanted = row_id + jnp.where(row_id < HALF, p0 * HALF, (p1 - 1) * HALF)
        acc = jnp.zeros((2 * HALF, 2 * COLS), F32)
        for b in range(0, BLOCKS, 4):
            pick = jnp.concatenate(
                [jnp.where(wanted == key[b + g], 1.0, 0.0).astype(BF16) for g in range(4)],
                axis=1,
            )
            vals = jnp.concatenate([bmat[b + g] for g in range(4)], axis=1)
            acc = acc + lax.dot_general(pick, vals, NT, preferred_element_type=F32)
        low = acc[:, :COLS].reshape(2, WIDE, 8, COLS)
        high = acc[:, COLS:].reshape(2, WIDE, 8, COLS)
        both = jnp.concatenate([low, high], axis=2).astype(BF16)
        msg[p0] = both[0]
        msg[p1] = both[1]
        narrow_copy(d).start()

        @pl.when(r < NARROW // 2 - 1)
        def _():
            narrow_copy(d + 1).start()

    send_big(SENT_SORT, SENT_NARROW)
    n1[:, n] = msg[n]
    for d in range(1, NARROW):
        narrow_copy(d).wait()
    wide = []
    for d in range(1, WIDE):
        q = lax.rem(w + d, WIDE)
        c = pltpu.make_async_remote_copy(
            n1.at[q], w2.at[w], wi_s.at[d], wi_r.at[d], device_id=(q, n), device_id_type=MESH
        )
        c.start()
        wide.append(c)
    w2[w] = n1[w]
    send_big(SENT_NARROW, len(ORDER))

    for c in slot_wide:
        c.wait()

    cells = s2[...].reshape(DEVICES, COLS).astype(BF16)
    ROWS = 256
    sub2 = lax.broadcasted_iota(I32, (ROWS, COLS), 0)
    lane2 = lax.broadcasted_iota(I32, (ROWS, COLS), 1)

    @pl.loop(0, 2048 // ROWS)
    def _(r):
        own = jnp.where(lane2 == r * (ROWS // 16) + (sub2 >> 4), 1.0, 0.0).astype(BF16)
        mine = jnp.dot(own, cells, preferred_element_type=F32)
        for j in range(4):
            one = jnp.where(lane2 == 8 * (sub2 & 7) + 4 * ((sub2 >> 3) & 1) + j, mine, 0.0).astype(BF16)
            cell = jnp.dot(one, ones, preferred_element_type=F32)
            cell = cell.astype(I32) + SLOTS // 2
            for k in range(SLOTS // COLS):
                hot[j, pl.ds(r * ROWS, ROWS), k * COLS : (k + 1) * COLS] = jnp.where(
                    cell == lane2 + k * COLS, 1.0, 0.0
                ).astype(BF16)

    for c in wide:
        c.wait()
    eye = jnp.where(sub == lane, 1.0, 0.0).astype(BF16)
    vals = w2[...].reshape(2048, COLS)
    turned = lax.dot_general(eye, vals, NT, preferred_element_type=F32).astype(BF16)
    total = jnp.zeros((NFLUX, SLOTS), F32)
    for j in range(4):
        total = total + jnp.dot(
            turned[j * NFLUX : (j + 1) * NFLUX], hot[j], preferred_element_type=F32
        )
    ocean[...] = total

    for p in range(RAW):
        big(p).wait_send()
    for p in range(RAW, 15):
        big(p).wait()


def final_kernel(sel, pool, cells, out, ocean, sem, cell_sem):
    def put(s):
        return pltpu.make_async_copy(pool.at[sel[s]], out.at[s], sem.at[s])

    for s in range(BLOCKS):
        put(s).start()
    last = pltpu.make_async_copy(cells, ocean, cell_sem)
    last.start()
    for s in range(BLOCKS):
        put(s).wait()
    last.wait()


def per_device(state, group_of, w_in, w_out, w_flux, owner, ocean_slot, remap_weight):
    vmem, hbm, smem = (
        pl.BlockSpec(memory_space=pltpu.VMEM),
        pl.BlockSpec(memory_space=pltpu.HBM),
        pl.BlockSpec(memory_space=pltpu.SMEM),
    )
    dma = pltpu.SemaphoreType.DMA
    pool, ocean, sel = pl.pallas_call(
        main_kernel,
        out_shape=(
            pltpu.VMEM((STAY + WIDE, DEPTH, COLS), BF16),
            pltpu.VMEM((NFLUX, SLOTS), F32),
            pltpu.SMEM((BLOCKS,), I32),
        ),
        in_specs=[smem, hbm, hbm, hbm, hbm, vmem, vmem, vmem],
        out_specs=(vmem, vmem, smem),
        scratch_shapes=[
            pltpu.VMEM((BLOCKS, DEPTH, COLS), BF16),
            pltpu.VMEM((RAW, DEPTH, COLS), BF16),
            pltpu.VMEM((MOVE, DEPTH, COLS), BF16),
            pltpu.VMEM((15, DEPTH, COLS), BF16),
            pltpu.VMEM((DEPTH, DEPTH), BF16),
            pltpu.VMEM((DEPTH + NFLUX, DEPTH), BF16),
            pltpu.VMEM((DEPTH, GROUP * COLS), BF16),
            pltpu.VMEM((MOVE, NFLUX, COLS), F32),
            pltpu.VMEM((15, NFLUX, COLS), BF16),
            pltpu.VMEM((STAY + WIDE, NFLUX, COLS), F32),
            pltpu.VMEM((WIDE, NFLUX, COLS), BF16),
            pltpu.VMEM((BLOCKS, 1, COLS), I32),
            pltpu.VMEM((BLOCKS, 1, COLS), I32),
            pltpu.VMEM((BLOCKS, 2 * COLS, COLS), BF16),
            pltpu.VMEM((NARROW, WIDE, 16, COLS), BF16),
            pltpu.VMEM((WIDE, NARROW, 16, COLS), BF16),
            pltpu.VMEM((WIDE, NARROW, 16, COLS), BF16),
            pltpu.VMEM((COLS, COLS), F32),
            pltpu.VMEM((COLS, COLS), F32),
            pltpu.VMEM((NARROW, WIDE, COLS), F32),
            pltpu.VMEM((NARROW, WIDE, COLS), F32),
            pltpu.VMEM((WIDE, NARROW, COLS), F32),
            pltpu.VMEM((WIDE, NARROW, COLS), F32),
            pltpu.VMEM((4, 2048, SLOTS), BF16),
            pltpu.SMEM((BLOCKS,), I32),
            pltpu.SMEM((16,), I32),
            pltpu.SMEM((17,), I32),
            pltpu.SMEM((15,), I32),
            pltpu.SMEM((BLOCKS,), I32),
            pltpu.SMEM((BLOCKS + 1,), I32),
            dma((11,)),
            dma((15,)),
            dma((15,)),
            dma((15,)),
            dma((15,)),
            dma((NARROW,)),
            dma((NARROW,)),
            dma((WIDE,)),
            dma((WIDE,)),
            dma((NARROW,)),
            dma((NARROW,)),
            dma((WIDE,)),
            dma((WIDE,)),
        ],
        compiler_params=pltpu.CompilerParams(
            collective_id=1, has_side_effects=True, vmem_limit_bytes=50 * 2**20
        ),
        name="physics",
    )(
        group_of,
        state,
        w_in,
        w_out,
        w_flux,
        owner.reshape(BLOCKS, 1, COLS),
        ocean_slot.reshape(BLOCKS, 1, COLS),
        remap_weight.reshape(BLOCKS, 1, COLS),
    )
    return pl.pallas_call(
        final_kernel,
        out_shape=(
            jax.ShapeDtypeStruct((BLOCKS, DEPTH, COLS), BF16),
            jax.ShapeDtypeStruct((NFLUX, SLOTS), F32),
        ),
        in_specs=[smem, vmem, vmem],
        out_specs=(hbm, hbm),
        scratch_shapes=[dma((BLOCKS,)), dma],
        compiler_params=pltpu.CompilerParams(vmem_limit_bytes=2 * 2**20),
        name="assemble",
    )(sel, pool, ocean)


def solution(mesh):
    rows = P(("wide", "narrow"))
    in_specs = (P(("wide", "narrow"), None, None), P(), P(), P(), P(), P(("wide", "narrow"), None), rows, rows)
    out_specs = (P(("wide", "narrow"), None, None), P(None, ("wide", "narrow")))
    return jax.shard_map(
        per_device, mesh=mesh, in_specs=in_specs, out_specs=out_specs, check_vma=False
    )
```

```python
import functools

import jax
import jax.numpy as jnp
from jax import lax
from jax.experimental import pallas as pl
from jax.experimental.pallas import tpu as pltpu
from jax.sharding import PartitionSpec as P

F32, BF16, I32 = jnp.float32, jnp.bfloat16, jnp.int32
MESH = pl.DeviceIdType.MESH
NT = (((1,), (1,)), ((), ()))

BLOCKS, DEPTH, COLS = 32, 1024, 128
NFLUX, SLOTS = 32, 512
WIDE, NARROW, SIDE = 16, 8, 4
DEVICES = WIDE * NARROW
MOVE, STAY = 8, 24
GROUP = 4
CHUNK = 256
PIECE = 128
ITEMS = (
    (1, 0), (3, 0), (0, 1), (0, 3), (1, 1), (3, 3), (1, 3), (3, 1),
    (2, 2), (2, 1), (2, 3), (1, 2), (3, 2), (2, 0), (0, 2),
)
CODES = tuple(dz * SIDE + dy for dy, dz in ITEMS)
RAW = 4
PARTS = 8
ORDER = [(p, part) for part in range(PARTS) for p in range(4, 8)]
ORDER += [(p, part) for part in range(PARTS) for p in range(8, 15)]
SENT = (32, 40, 46, 52, 58, 64, 68, 72)
SENT_LAST = 74
SENT_SORT = 76
SENT_NARROW = 80


def silu(v):
    return v / (1.0 + jnp.exp(-v))


def main_kernel(
    group_of, state, w_in_hbm, w_out_hbm, w_flux_hbm, owner, slot, weight,
    pool, ocean, sel,
    xs, rx, ys, send, w_in, w_out, hid, fm, fs, fp, fr, key, jrank, bmat, msg, n1, w2, ahead_of, cells_of, sl, s1, s1t, s2, hot,
    code_t, slot_t, next_t, rank_t, order_t, local_t,
    load_sem, big_s, big_r, fl_s, fl_r, na_s, na_r, wi_s, wi_r, sn_s, sn_r, sw_s, sw_r,
):
    w, n = lax.axis_index("wide"), lax.axis_index("narrow")
    y, z = lax.rem(w, SIDE), lax.div(w, SIDE)
    loads = [
        pltpu.make_async_copy(w_in_hbm, w_in, load_sem.at[0]),
        pltpu.make_async_copy(w_out_hbm, w_out.at[pl.ds(0, DEPTH)], load_sem.at[9]),
        pltpu.make_async_copy(w_flux_hbm, w_out.at[pl.ds(DEPTH, NFLUX)], load_sem.at[10]),
    ]
    for i in range(8):
        loads.append(
            pltpu.make_async_copy(
                state.at[pl.ds(4 * i, 4)], xs.at[pl.ds(4 * i, 4)], load_sem.at[1 + i]
            )
        )
    for c in loads[3:]:
        c.start()
    for c in loads[:3]:
        c.start()

    def target(p):
        dy, dz = ITEMS[p]
        return (lax.rem(z + dz, SIDE) * SIDE + lax.rem(y + dy, SIDE), n)

    wide_peers = [(lax.rem(w + d, WIDE), n) for d in range(1, WIDE)]
    narrow_peers = [(w, lax.rem(n + d, NARROW)) for d in range(1, NARROW)]
    barrier = pltpu.get_barrier_semaphore()
    for peer in wide_peers + narrow_peers:
        pl.semaphore_signal(barrier, inc=1, device_id=peer, device_id_type=MESH)

    base_row = (w * NARROW + n) * BLOCKS

    def scan_slots(s, found):
        t = lax.div(group_of[base_row + s], NARROW * BLOCKS)
        dy = lax.rem(lax.rem(t, SIDE) - y + SIDE, SIDE)
        dz = lax.rem(lax.div(t, SIDE) - z + SIDE, SIDE)
        src = lax.rem(2 * w - t + 2 * WIDE, WIDE)
        ry = lax.rem(y - lax.rem(src, SIDE) + SIDE, SIDE)
        rz = lax.rem(z - lax.div(src, SIDE) + SIDE, SIDE)
        code = dz * SIDE + dy
        code_t[s] = code
        sel[s] = STAY + rz * SIDE + ry
        return tuple(jnp.where(code == CODES[p], s, found[p]) for p in range(15))

    found = lax.fori_loop(0, BLOCKS, scan_slots, (jnp.int32(-1),) * 15)
    nxt = jnp.int32(15)
    slot_t[15] = jnp.int32(0)
    next_t[15] = jnp.int32(15)
    next_t[16] = jnp.int32(15)
    for p in reversed(range(15)):
        nxt = jnp.where(found[p] >= 0, p, nxt)
        next_t[p] = nxt
        slot_t[p] = jnp.maximum(found[p], 0)
    count = jnp.int32(0)
    for p in range(RAW, 15):
        rank_t[p] = jnp.minimum(count, MOVE - 1)
        count = count + jnp.where(found[p] >= 0, 1, 0)

    def walk_movers(k, p):
        order_t[k] = slot_t[p]
        return next_t[p + 1]

    lax.fori_loop(0, MOVE, walk_movers, next_t[RAW])

    def back_locals(i, nx):
        s = BLOCKS - 1 - i
        nx = jnp.where(code_t[s] == 0, s, nx)
        local_t[s] = nx
        return nx

    local_t[BLOCKS] = jnp.int32(BLOCKS - 1)
    lax.fori_loop(0, BLOCKS, back_locals, jnp.int32(BLOCKS - 1))

    def number_locals(s, cnt):
        stays = code_t[s] == 0
        sel[s] = jnp.where(stays, jnp.minimum(cnt, STAY - 1), sel[s])
        return cnt + jnp.where(stays, 1, 0)

    lax.fori_loop(0, BLOCKS, number_locals, jnp.int32(0))

    def walk_locals(k, s):
        order_t[MOVE + k] = s
        return local_t[s + 1]

    lax.fori_loop(0, STAY, walk_locals, local_t[0])

    sub = lax.broadcasted_iota(I32, (COLS, COLS), 0)
    lane = lax.broadcasted_iota(I32, (COLS, COLS), 1)
    before = jnp.where(sub < lane, 1.0, 0.0).astype(BF16)
    ones = jnp.full((COLS, COLS), 1.0, BF16)

    ahead_of[...] = jnp.zeros((COLS, COLS), F32)
    cells_of[...] = jnp.zeros((COLS, COLS), F32)

    def place(i):
        base, table = ahead_of[...], cells_of[...]
        for g in range(4):
            s = 4 * i + g
            o = owner[s]
            row = (o & (NARROW - 1)) * WIDE + (o >> 3)
            member = jnp.where(sub == row, 1.0, 0.0)
            member16 = member.astype(BF16)
            ahead = jnp.dot(member16, before, preferred_element_type=F32)
            count = jnp.dot(member16, ones, preferred_element_type=F32)
            rank = jnp.sum((ahead + base) * member, axis=0, keepdims=True).astype(I32)
            base = base + count
            key[s] = row * 8 + (rank >> 3)
            jrank[s] = rank & 7
            cell = (slot[s] - SLOTS // 2).astype(F32)
            ranked = jnp.where(sub == rank, cell, 0.0).astype(BF16)
            table = table + lax.dot_general(member16, ranked, NT, preferred_element_type=F32)
        ahead_of[...] = base
        cells_of[...] = table

    def slots_out():
        sl[...] = cells_of[...].reshape(NARROW, WIDE, COLS)
        for c in slot_narrow:
            c.start()
        s1[n] = sl[n]

    slot_narrow = []
    for d in range(1, NARROW):
        p = lax.rem(n + d, NARROW)
        c = pltpu.make_async_remote_copy(
            sl.at[p], s1.at[n], sn_s.at[d], sn_r.at[d], device_id=(w, p), device_id_type=MESH
        )
        slot_narrow.append(c)

    def big(p, part=None):
        rows = pl.ds(0, DEPTH) if part is None else pl.ds(part * PIECE, PIECE)
        return pltpu.make_async_remote_copy(
            send.at[p, rows],
            rx.at[p, rows] if p < RAW else pool.at[STAY + CODES[p], rows],
            big_s.at[p],
            big_r.at[p],
            device_id=target(p),
            device_id_type=MESH,
        )

    def flux_copy(p):
        return pltpu.make_async_remote_copy(
            fs.at[p], fr.at[CODES[p]], fl_s.at[p], fl_r.at[p],
            device_id=target(p), device_id_type=MESH,
        )

    def fill(ps):
        for p in ps:
            fs[p] = fm[rank_t[p]].astype(BF16)
        for p in ps:
            send[p] = ys[rank_t[p]]

    def send_big(first, last):
        for p, part in ORDER[first:last]:
            big(p, part).start()

    slot_wide = []
    for d in range(1, WIDE):
        q = lax.rem(w + d, WIDE)
        slot_wide.append(
            pltpu.make_async_remote_copy(
                s1t.at[q], s2.at[w], sw_s.at[d], sw_r.at[d], device_id=(q, n), device_id_type=MESH
            )
        )

    for c in loads[3:]:
        c.wait()
    for p in range(RAW):
        send[p] = xs[slot_t[p]]
    pl.semaphore_wait(barrier, len(wide_peers) + len(narrow_peers))
    for part in range(PARTS):
        for p in range(RAW):
            big(p, part).start()
    for c in loads[:3]:
        c.wait()

    def columns(v, g):
        return v[:, g * COLS : (g + 1) * COLS]

    def compute(x, put_flux, put_rows):
        for m in range(DEPTH // CHUNK):
            rows = pl.ds(m * CHUNK, CHUNK)
            hid[rows, :] = silu(
                jnp.dot(w_in[rows, :], x, preferred_element_type=F32)
            ).astype(BF16)
        h = hid[...]
        for m in range(DEPTH // CHUNK):
            last = m == DEPTH // CHUNK - 1
            rows = pl.ds(m * CHUNK, CHUNK)
            both = jnp.dot(
                w_out[pl.ds(m * CHUNK, CHUNK + (NFLUX if last else 0)), :],
                h,
                preferred_element_type=F32,
            )
            fresh = both[:CHUNK] + x[m * CHUNK : (m + 1) * CHUNK].astype(F32)
            put_rows(rows, fresh.astype(BF16))
            if last:
                put_flux(both[CHUNK:])

    def gathered(q):
        return jnp.concatenate([xs[order_t[GROUP * q + g]] for g in range(GROUP)], axis=1)

    def moved(q):
        def put_flux(f):
            for g in range(GROUP):
                fm[GROUP * q + g] = columns(f, g)

        def put_rows(rows, fresh):
            for g in range(GROUP):
                ys[GROUP * q + g, rows] = columns(fresh, g)

        place(q)
        compute(gathered(q), put_flux, put_rows)

    def send_moved(ps, first, last):
        fill(ps)
        for p in ps:
            flux_copy(p).start()
        send_big(first, last)

    moved(0)
    send_moved(range(4, 8), 0, SENT[0])
    moved(1)
    send_moved(range(8, 15), SENT[0], SENT[1])

    @pl.loop(0, STAY // GROUP)
    def _(k):
        def put_flux(f):
            for g in range(GROUP):
                fp[GROUP * k + g] = columns(f, g)

        def put_rows(rows, fresh):
            for g in range(GROUP):
                pool[GROUP * k + g, rows] = columns(fresh, g)

        place(k + 2)
        compute(gathered(k + 2), put_flux, put_rows)
        for step in range(STAY // GROUP):

            @pl.when(k == step)
            def _(step=step):
                send_big(SENT[step + 1], SENT[step + 2])

    slots_out()

    for p in range(RAW):
        big(p).wait_recv()

    def raw_flux(f):
        for p in range(RAW):
            fp[STAY + CODES[p]] = columns(f, p)

    def raw_rows(rows, fresh):
        for p in range(RAW):
            pool[STAY + CODES[p], rows] = columns(fresh, p)

    compute(jnp.concatenate([rx[p] for p in range(RAW)], axis=1), raw_flux, raw_rows)

    for c in slot_narrow:
        c.wait()
    for p in range(NARROW):
        s1t[:, p, :] = s1[p]
    s2[w] = s1t[w]
    for c in slot_wide:
        c.start()
    send_big(SENT[-1], SENT_LAST)

    for p in range(RAW, 15):
        flux_copy(p).wait()
        fp[STAY + CODES[p]] = fr[CODES[p]].astype(F32)
    send_big(SENT_LAST, SENT_SORT)

    @pl.loop(0, BLOCKS)
    def _(s):
        f = fp[sel[s]] * weight[s]
        j = jrank[s]
        spread = jnp.concatenate([jnp.where(j == k, f, 0.0) for k in range(8)], axis=0)
        bmat[s] = spread.astype(BF16)

    HALF = WIDE * 8
    row_id = lax.broadcasted_iota(I32, (2 * HALF, COLS), 0)

    def narrow_copy(d):
        p = lax.rem(n + d, NARROW)
        return pltpu.make_async_remote_copy(
            msg.at[p], n1.at[:, n], na_s.at[d], na_r.at[d], device_id=(w, p), device_id_type=MESH
        )

    @pl.loop(0, NARROW // 2)
    def _(r):
        d = 2 * r + 1
        p0, p1 = lax.rem(n + d, NARROW), lax.rem(n + d + 1, NARROW)
        wanted = row_id + jnp.where(row_id < HALF, p0 * HALF, (p1 - 1) * HALF)
        acc = jnp.zeros((2 * HALF, 2 * COLS), F32)
        for b in range(0, BLOCKS, 4):
            pick = jnp.concatenate(
                [jnp.where(wanted == key[b + g], 1.0, 0.0).astype(BF16) for g in range(4)],
                axis=1,
            )
            vals = jnp.concatenate([bmat[b + g] for g in range(4)], axis=1)
            acc = acc + lax.dot_general(pick, vals, NT, preferred_element_type=F32)
        low = acc[:, :COLS].reshape(2, WIDE, 8, COLS)
        high = acc[:, COLS:].reshape(2, WIDE, 8, COLS)
        both = jnp.concatenate([low, high], axis=2).astype(BF16)
        msg[p0] = both[0]
        msg[p1] = both[1]
        narrow_copy(d).start()

        @pl.when(r < NARROW // 2 - 1)
        def _():
            narrow_copy(d + 1).start()

    send_big(SENT_SORT, SENT_NARROW)
    n1[:, n] = msg[n]
    for d in range(1, NARROW):
        narrow_copy(d).wait()
    wide = []
    for d in range(1, WIDE):
        q = lax.rem(w + d, WIDE)
        c = pltpu.make_async_remote_copy(
            n1.at[q], w2.at[w], wi_s.at[d], wi_r.at[d], device_id=(q, n), device_id_type=MESH
        )
        c.start()
        wide.append(c)
    w2[w] = n1[w]
    send_big(SENT_NARROW, len(ORDER))

    for c in slot_wide:
        c.wait()

    cells = s2[...].reshape(DEVICES, COLS).astype(BF16)
    ROWS = 256
    sub2 = lax.broadcasted_iota(I32, (ROWS, COLS), 0)
    lane2 = lax.broadcasted_iota(I32, (ROWS, COLS), 1)

    @pl.loop(0, 2048 // ROWS)
    def _(r):
        own = jnp.where(lane2 == r * (ROWS // 16) + (sub2 >> 4), 1.0, 0.0).astype(BF16)
        mine = jnp.dot(own, cells, preferred_element_type=F32)
        for j in range(4):
            one = jnp.where(lane2 == 8 * (sub2 & 7) + 4 * ((sub2 >> 3) & 1) + j, mine, 0.0).astype(BF16)
            cell = jnp.dot(one, ones, preferred_element_type=F32)
            cell = cell.astype(I32) + SLOTS // 2
            for k in range(SLOTS // COLS):
                hot[j, pl.ds(r * ROWS, ROWS), k * COLS : (k + 1) * COLS] = jnp.where(
                    cell == lane2 + k * COLS, 1.0, 0.0
                ).astype(BF16)

    for c in wide:
        c.wait()
    eye = jnp.where(sub == lane, 1.0, 0.0).astype(BF16)
    vals = w2[...].reshape(2048, COLS)
    turned = lax.dot_general(eye, vals, NT, preferred_element_type=F32).astype(BF16)
    total = jnp.zeros((NFLUX, SLOTS), F32)
    for j in range(4):
        total = total + jnp.dot(
            turned[j * NFLUX : (j + 1) * NFLUX], hot[j], preferred_element_type=F32
        )
    ocean[...] = total

    for p in range(RAW):
        big(p).wait_send()
    for p in range(RAW, 15):
        big(p).wait()


def final_kernel(sel, pool, cells, out, ocean, sem, cell_sem):
    def put(s):
        return pltpu.make_async_copy(pool.at[sel[s]], out.at[s], sem.at[s])

    for s in range(BLOCKS):
        put(s).start()
    last = pltpu.make_async_copy(cells, ocean, cell_sem)
    last.start()
    for s in range(BLOCKS):
        put(s).wait()
    last.wait()


def per_device(state, group_of, w_in, w_out, w_flux, owner, ocean_slot, remap_weight):
    vmem, hbm, smem = (
        pl.BlockSpec(memory_space=pltpu.VMEM),
        pl.BlockSpec(memory_space=pltpu.HBM),
        pl.BlockSpec(memory_space=pltpu.SMEM),
    )
    dma = pltpu.SemaphoreType.DMA
    pool, ocean, sel = pl.pallas_call(
        main_kernel,
        out_shape=(
            pltpu.VMEM((STAY + WIDE, DEPTH, COLS), BF16),
            pltpu.VMEM((NFLUX, SLOTS), F32),
            pltpu.SMEM((BLOCKS,), I32),
        ),
        in_specs=[smem, hbm, hbm, hbm, hbm, vmem, vmem, vmem],
        out_specs=(vmem, vmem, smem),
        scratch_shapes=[
            pltpu.VMEM((BLOCKS, DEPTH, COLS), BF16),
            pltpu.VMEM((RAW, DEPTH, COLS), BF16),
            pltpu.VMEM((MOVE, DEPTH, COLS), BF16),
            pltpu.VMEM((15, DEPTH, COLS), BF16),
            pltpu.VMEM((DEPTH, DEPTH), BF16),
            pltpu.VMEM((DEPTH + NFLUX, DEPTH), BF16),
            pltpu.VMEM((DEPTH, GROUP * COLS), BF16),
            pltpu.VMEM((MOVE, NFLUX, COLS), F32),
            pltpu.VMEM((15, NFLUX, COLS), BF16),
            pltpu.VMEM((STAY + WIDE, NFLUX, COLS), F32),
            pltpu.VMEM((WIDE, NFLUX, COLS), BF16),
            pltpu.VMEM((BLOCKS, 1, COLS), I32),
            pltpu.VMEM((BLOCKS, 1, COLS), I32),
            pltpu.VMEM((BLOCKS, 2 * COLS, COLS), BF16),
            pltpu.VMEM((NARROW, WIDE, 16, COLS), BF16),
            pltpu.VMEM((WIDE, NARROW, 16, COLS), BF16),
            pltpu.VMEM((WIDE, NARROW, 16, COLS), BF16),
            pltpu.VMEM((COLS, COLS), F32),
            pltpu.VMEM((COLS, COLS), F32),
            pltpu.VMEM((NARROW, WIDE, COLS), F32),
            pltpu.VMEM((NARROW, WIDE, COLS), F32),
            pltpu.VMEM((WIDE, NARROW, COLS), F32),
            pltpu.VMEM((WIDE, NARROW, COLS), F32),
            pltpu.VMEM((4, 2048, SLOTS), BF16),
            pltpu.SMEM((BLOCKS,), I32),
            pltpu.SMEM((16,), I32),
            pltpu.SMEM((17,), I32),
            pltpu.SMEM((15,), I32),
            pltpu.SMEM((BLOCKS,), I32),
            pltpu.SMEM((BLOCKS + 1,), I32),
            dma((11,)),
            dma((15,)),
            dma((15,)),
            dma((15,)),
            dma((15,)),
            dma((NARROW,)),
            dma((NARROW,)),
            dma((WIDE,)),
            dma((WIDE,)),
            dma((NARROW,)),
            dma((NARROW,)),
            dma((WIDE,)),
            dma((WIDE,)),
        ],
        compiler_params=pltpu.CompilerParams(
            collective_id=1, has_side_effects=True, vmem_limit_bytes=50 * 2**20
        ),
        name="physics",
    )(
        group_of,
        state,
        w_in,
        w_out,
        w_flux,
        owner.reshape(BLOCKS, 1, COLS),
        ocean_slot.reshape(BLOCKS, 1, COLS),
        remap_weight.reshape(BLOCKS, 1, COLS),
    )
    return pl.pallas_call(
        final_kernel,
        out_shape=(
            jax.ShapeDtypeStruct((BLOCKS, DEPTH, COLS), BF16),
            jax.ShapeDtypeStruct((NFLUX, SLOTS), F32),
        ),
        in_specs=[smem, vmem, vmem],
        out_specs=(hbm, hbm),
        scratch_shapes=[dma((BLOCKS,)), dma],
        compiler_params=pltpu.CompilerParams(vmem_limit_bytes=2 * 2**20),
        name="assemble",
    )(sel, pool, ocean)


def solution(mesh):
    rows = P(("wide", "narrow"))
    in_specs = (P(("wide", "narrow"), None, None), P(), P(), P(), P(), P(("wide", "narrow"), None), rows, rows)
    out_specs = (P(("wide", "narrow"), None, None), P(None, ("wide", "narrow")))
    return jax.shard_map(
        per_device, mesh=mesh, in_specs=in_specs, out_specs=out_specs, check_vma=False
    )
```
